32 devices in a mesh: cent: 8 (over y, x, core), rep: 4 (over z).
Axes of the slice: x: 2, y: 2, z: 4, core: 2. Of those that a mesh axis runs over, the one named last changes fastest.
Arguments:
- points: bfloat16 [16384, 1024], P(('cent', 'rep')), may hold values from -6 to 6
- centroids: bfloat16 [4096, 1024], P('cent'), may hold values from -6 to 6
- owners: int32 [16384, 2], P(('cent', 'rep')), may hold values from 0 to 7, all different within a row; in each aligned block of 512 rows (0 to 511, 512 to 1023, ...) at most 320 rows name the same one
- blocks: int32 [16384, 2, 4], P(('cent', 'rep')), may hold values from 0 to 7, all different within a row
- duals: float32 [4096], P('cent'), may hold values from -1 to 1
Outputs:
- new_centroids: bfloat16 [4096, 1024], P('cent')
- duals_out: float32 [4096], P('cent')
The draws below stay inside these ranges and needn't reach their ends.
Inputs may be any that keep to these rules, and one draw needn't show every extreme that they name: `owners`: each point names 2 different owner shards; among the points of one device no shard is named more than 320 times, a bound that some block reaches. `blocks`: the 4 block numbers that a point names within one owner shard differ.
All inputs are finite; a program needn't handle non-finite values.
Results may differ from the reference program's by a relative error of at most 0.012.
The reference program's roundings to bfloat16 on the way count: a program that leaves them out, or rounds other values in their place, can miss the bound.
Values may be sent and summed in bfloat16 or wider, within the bound.
A program may use at most 64 MiB of HBM per device.

```python
import math
import jax
import jax.numpy as jnp
import numpy as np
from jax import lax

EMBED_WIDTH = 1024
P_DEV = 512
K_DEV = 512
BLOCKS_DEV = 8
CAND = 4
ROUTES = 2
SINK = 3
ITERS = 2
SHARDS = 8
CAP = 320
POINTS = 16384
CLUSTERS = 4096
N_CENT = 8
N_REP = 4


def block_scale(rng, extent, pieces, least, high):
    factor_of = 1.0
    for axis_at, shards_of in pieces:
        draws = jax.random.uniform(jax.random.fold_in(jax.random.fold_in(rng, 6), axis_at), (shards_of,), jnp.float32, least / len(pieces), high / len(pieces))
        factor_of = factor_of * jnp.repeat(jnp.exp(draws), extent[axis_at] // shards_of).reshape((-1,) + (1,) * (len(extent) - 1 - axis_at))
    return factor_of


def distinct(own_key, rows, number_of, top, lift):
    ranking = jax.random.permutation(jax.random.fold_in(own_key, 1), number_of)
    boost = ranking
    for power in range(3):
        boost = boost * boost // number_of
    boost = boost * lift // number_of
    lots = jax.random.randint(jax.random.fold_in(own_key, 2), (rows, number_of), 0, 4096) + boost
    holders = jax.random.permutation(jax.random.fold_in(own_key, 3), rows)[jnp.arange(number_of) % rows]
    lots = jnp.where(jnp.arange(rows)[:, None] == holders[None, :], 1 << 14, lots)
    merit = lots * number_of + jnp.arange(number_of)
    return lax.top_k(merit.astype(jnp.int32), top)[1].astype(jnp.int32)


def deal_out(rng, own, number, rows, count, top, most, lean):
    order = jax.random.permutation(rng, count)
    crowded, common = shares(count, rows * top, most, lean, True), shares(count, rows * top, most, lean, False)
    places = jnp.arange(count)

    def named(tallies, rotation):
        used = int((tallies > 0).sum())
        fixed = max(1, used // 4)
        shifted = fixed + (places - fixed + rotation * (used - fixed)) % max(1, count - fixed)
        return jnp.zeros((count,), jnp.int32).at[order[jnp.where(places < fixed, places, shifted)]].set(jnp.asarray(tallies, jnp.int32))

    tallies = jnp.where(number % 4 == 0, named(crowded, number // 4), named(common, number - number // 4 - 1))
    mixed = jax.random.permutation(jax.random.fold_in(own, 3), count)
    source_of, taker = mixed[0:count // 2 * 2:2], mixed[1:count // 2 * 2:2]
    room = jnp.minimum(tallies[source_of] - 1, most - tallies[taker]) // 2
    room = jnp.where((source_of == order[0]) | (taker == order[0]) | (tallies[taker] == 0), 0, jnp.maximum(room, 0))
    shifted = jax.random.randint(jax.random.fold_in(own, 4), (count // 2,), 0, 1 << 20) % (room + 1)
    tallies = tallies.at[source_of].add(-shifted).at[taker].add(shifted)
    members = jnp.searchsorted(jnp.cumsum(tallies), jnp.arange(rows * top), side="right").astype(jnp.int32)
    grid = members.reshape(top, rows).T
    grid = grid[jax.random.permutation(jax.random.fold_in(own, 1), rows)]
    rotation = jax.random.randint(jax.random.fold_in(own, 2), (rows, 1), 0, top)
    return jnp.take_along_axis(grid, (jnp.arange(top)[None, :] + rotation) % top, axis=1)


def shares(amount, total, most, slope, full):
    loads = [(1 << 20) // math.isqrt(grade ** slope) + 1 for grade in range(1, amount + 1)]
    largest = most if full else min(most, max(-(-total // amount), total * loads[0] // sum(loads)))
    least = 1 if total - largest >= amount - 1 else 0
    counts, spare = [largest] + [least] * (amount - 1), total - largest - least * (amount - 1)
    while spare > 0:
        free = [i for i in range(1, amount) if counts[i] < largest] or [i for i in range(1, amount) if counts[i] < most]
        pool, left = sum([loads[i] for i in free]), spare
        for i in free:
            extra = min(most - counts[i], max(1, left * loads[i] // pool), spare)
            counts[i] = counts[i] + extra
            spare = spare - extra
    return np.array(counts)


def bell_draw(rng, shape, deviation, bound, split=(), held_as=jnp.bfloat16):
    entries = jax.random.normal(rng, shape, jnp.float32) * deviation
    if len(split) > 0:
        entries = block_scale(rng, shape, split, -0.22, 0.18) * entries
    return jnp.clip(entries, min=-bound, max=bound).astype(held_as)


def setup_inputs(seed: int = 0) -> dict:
    arg_keys = jax.random.split(jax.random.key(seed), 6)
    points = bell_draw(arg_keys[0], (POINTS, EMBED_WIDTH), 1.0, 6.0, ((0, 32),))
    centroids = bell_draw(arg_keys[1], (CLUSTERS, EMBED_WIDTH), 1.0, 6.0, ((0, 8),))
    owners_keys = jax.random.split(jax.random.fold_in(arg_keys[2], 1), POINTS // P_DEV)
    owners_turns = jax.random.permutation(jax.random.fold_in(arg_keys[2], 3), POINTS // P_DEV)
    owners = jax.vmap(lambda own, number: deal_out(jax.random.fold_in(arg_keys[2], 2), own, number, P_DEV, SHARDS, ROUTES, CAP, 1))(owners_keys, owners_turns).reshape((POINTS, ROUTES))
    blocks = distinct(arg_keys[3], POINTS * ROUTES, BLOCKS_DEV, CAND, 0).reshape((POINTS, ROUTES, CAND))
    duals = jnp.clip(jax.random.uniform(arg_keys[4], (CLUSTERS,), jnp.float32, -1.0, 1.0) * block_scale(arg_keys[4], (CLUSTERS,), ((0, 8),), -0.4, 0.0), -1.0, 1.0)
    return {"points": points, "centroids": centroids, "owners": owners, "blocks": blocks, "duals": duals}


softness_factor = 0.02
EPSILON = 1e-06

def normalize(values):
    widened = values.astype(jnp.float32)
    return (widened * lax.rsqrt(lax.optimization_barrier(jnp.mean(widened * widened, axis=-1, keepdims=True)) + EPSILON)).astype(jnp.bfloat16)

def reference(points, centroids, owners, blocks, duals):
    total_points = points.shape[0]
    route_count = total_points * ROUTES
    block_span = K_DEV // BLOCKS_DEV
    per_owner = N_CENT * N_REP * CAP
    target = P_DEV * N_REP / K_DEV
    unit_rows = normalize(points)
    flat_owner = owners.reshape(-1).astype(jnp.int32)
    flat_point = jnp.arange(route_count, dtype=jnp.int32) // ROUTES
    flat_blocks = blocks.reshape(route_count, CAND).astype(jnp.int32)
    shard_ids = jnp.arange(N_CENT, dtype=jnp.int32)
    owner_loads = lax.optimization_barrier(jnp.sum((flat_owner[None, :] == shard_ids[:, None]).astype(jnp.int32), axis=1))
    starts = jnp.cumsum(owner_loads) - owner_loads
    ordering = jnp.argsort(flat_owner, stable=True).astype(jnp.int32)
    offsets = jnp.arange(per_owner, dtype=jnp.int32)
    live_slots = offsets[None, :] < owner_loads[:, None]
    picked = ordering[jnp.clip(starts[:, None] + offsets[None, :], 0, route_count - 1)]
    picked = jnp.where(live_slots, picked, 0).astype(jnp.int32)
    member = jnp.any(flat_blocks[picked][:, :, :, None] == jnp.arange(BLOCKS_DEV, dtype=jnp.int32), axis=2)
    member = jnp.logical_and(member, live_slots[:, :, None]).astype(jnp.float32)
    live_float = live_slots.astype(jnp.float32)
    current = centroids
    duals_now = duals.reshape(N_CENT, K_DEV).astype(jnp.float32)
    for loop_counter in range(ITERS):
        centroid_unit = normalize(current).reshape(N_CENT, K_DEV, EMBED_WIDTH)

        def owner_kernel(inputs):
            chosen, block_marks, center_rows = inputs
            collected_rows = unit_rows[flat_point[chosen]]
            affinity_scores = lax.dot_general(collected_rows, center_rows, (((1,), (1,)), ((), ())), preferred_element_type=jnp.float32) / (EMBED_WIDTH * softness_factor)
            return jnp.exp(affinity_scores) * jnp.repeat(block_marks, block_span, axis=1)
        kernel = lax.map(owner_kernel, (picked, member, centroid_unit))
        for turn_index in range(SINK + 1):
            scaling = jnp.exp(duals_now)
            partial_rows = jnp.einsum('crk,ck->cr', kernel, scaling, precision=lax.Precision.HIGHEST)
            route_parts = jnp.zeros((route_count,), jnp.float32).at[picked.reshape(-1)].add(partial_rows.reshape(-1))
            inverse = 1.0 / lax.optimization_barrier(jnp.sum(route_parts.reshape(total_points, ROUTES), axis=1))
            row_scale = inverse[flat_point[picked]] * live_float
            if turn_index < SINK:
                column_mass = jnp.einsum('cr,crk->ck', row_scale, kernel, precision=lax.Precision.HIGHEST) * scaling
                duals_now = duals_now + jnp.log(2.0 * target) - jnp.log(column_mass + target)
        weights = (row_scale[:, :, None] * kernel * scaling[:, None, :]).astype(jnp.bfloat16)

        def owner_sums(inputs):
            chosen, weight_rows = inputs
            collected_rows = unit_rows[flat_point[chosen]]
            return lax.dot_general(weight_rows, collected_rows, (((0,), (0,)), ((), ())), preferred_element_type=jnp.float32)
        summed = lax.map(owner_sums, (picked, weights)).reshape(N_CENT * K_DEV, EMBED_WIDTH)
        current = normalize(summed)
    return (current, duals_now.reshape(-1))
```

```python
import functools

import jax
import jax.numpy as jnp
from jax import lax
from jax.experimental import pallas as pl
from jax.experimental.pallas import tpu as pltpu
from jax.sharding import PartitionSpec as P

BLOCKS_DEV = 8
CAND = 4
SINK = 3
ITERS = 2
LANES = 128
SUBLANES = 8
SUM_BLOCKS = 4
GROUP_PARTS = (1, 1, 2, 2, 2, 2, 2, 2, 1, 1)
MESH = pl.DeviceIdType.MESH
VMEM_LIMIT = 64000000


softness_factor = 0.02
EPSILON = 1e-06


def normalize(values):
    widened = values.astype(jnp.float32)
    return (
        widened * lax.rsqrt(jnp.mean(widened * widened, axis=-1, keepdims=True) + EPSILON)
    ).astype(jnp.bfloat16)


def candidate_mask(labels_in, block_span):
    member = jnp.any(
        labels_in[:, :, None] == jnp.arange(BLOCKS_DEV, dtype=jnp.int32)[None, None, :], axis=1
    )
    return jnp.repeat(member.astype(jnp.float32), block_span, axis=1)


def kernel_of(slot_rows, slot_mask, centroid_unit, feature_dimension):
    affinity_scores = lax.dot_general(
        slot_rows, centroid_unit, (((1,), (1,)), ((), ())), preferred_element_type=jnp.float32
    ) / (feature_dimension * softness_factor)
    return jnp.exp(affinity_scores) * slot_mask


def routed_body(points, centroids, owners, blocks, duals):
    point_rows, feature_dimension = points.shape
    shard_rows = centroids.shape[0]
    shards = lax.axis_size("cent")
    replicas = lax.axis_size("rep")
    routes = owners.shape[1]
    capacity = 5 * point_rows // shards
    block_span = shard_rows // BLOCKS_DEV
    target = point_rows * replicas / shard_rows
    unit_rows = normalize(points)
    flat_owner = owners.reshape(-1)
    flat_point = jnp.arange(point_rows * routes, dtype=jnp.int32) // routes
    onehot = (flat_owner[:, None] == jnp.arange(shards, dtype=jnp.int32)[None, :]).astype(jnp.int32)
    position = jnp.sum((jnp.cumsum(onehot, axis=0) - onehot) * onehot, axis=1)
    outgoing = (
        jnp.zeros((shards, capacity, feature_dimension), jnp.bfloat16)
        .at[flat_owner, position]
        .set(unit_rows[flat_point])
    )
    labels = (
        jnp.full((shards, capacity, CAND), -1, jnp.int32)
        .at[flat_owner, position]
        .set(blocks.reshape(-1, CAND))
    )
    first_unit = normalize(centroids)
    received_rows = (
        lax.all_to_all(outgoing, "cent", split_axis=0, concat_axis=0, tiled=True),
        lax.all_to_all(labels, "cent", split_axis=0, concat_axis=0, tiled=True),
    )
    slot_rows = received_rows[0].reshape(-1, feature_dimension)
    slot_mask = candidate_mask(received_rows[1].reshape(-1, CAND), block_span)
    first_kernel = kernel_of(slot_rows, slot_mask, first_unit, feature_dimension)
    current = centroids
    duals_now = duals
    for loop_counter in range(ITERS):
        if loop_counter == 0:
            kernel = first_kernel
        else:
            kernel = kernel_of(slot_rows, slot_mask, normalize(current), feature_dimension)
        for turn_index in range(SINK + 1):
            scaling = jnp.exp(duals_now)
            partial_rows = jnp.dot(kernel, scaling, precision=lax.Precision.HIGHEST).reshape(
                shards, capacity
            )
            returned = lax.all_to_all(partial_rows, "cent", split_axis=0, concat_axis=0, tiled=True)
            totals = jnp.sum(returned[flat_owner, position].reshape(point_rows, routes), axis=1)
            inverse = 1.0 / totals
            spread = (
                jnp.zeros((shards, capacity), jnp.float32)
                .at[flat_owner, position]
                .set(inverse[flat_point])
            )
            row_scale = lax.all_to_all(
                spread, "cent", split_axis=0, concat_axis=0, tiled=True
            ).reshape(-1)
            if turn_index < SINK:
                local_mass = jnp.dot(row_scale, kernel, precision=lax.Precision.HIGHEST) * scaling
                column_mass = lax.psum(local_mass, "rep")
                duals_now = duals_now + jnp.log(2.0 * target) - jnp.log(column_mass + target)
        weights = (row_scale[:, None] * kernel * scaling[None, :]).astype(jnp.bfloat16)
        share_sums = lax.psum_scatter(
            lax.dot_general(
                weights, slot_rows, (((0,), (0,)), ((), ())), preferred_element_type=jnp.float32
            ),
            "rep",
            scatter_dimension=0,
            tiled=True,
        )
        current = lax.all_gather(normalize(share_sums), "rep", axis=0, tiled=True)
    return (current, duals_now)


def fused_kernel(
    dims,
    points_ref,
    centroids_ref,
    owners_ref,
    blocks_ref,
    duals_ref,
    out_ref,
    duals_out_ref,
    units,
    marks_out,
    masks,
    kern,
    cunit,
    scale_cols,
    mass_cols,
    weights,
    sums,
    row_parts,
    col_parts,
    raw_out,
    raw_in,
    pair_out,
    pair_in,
    unit_send,
    unit_recv,
    mask_send,
    mask_recv,
    row_send,
    row_recv,
    col_send,
    col_recv,
    raw_send,
    raw_recv,
    pair_send,
    pair_recv,
    new_send,
    new_recv,
):
    shards, replicas, point_rows, shard_rows, features = dims
    span = shard_rows // BLOCKS_DEV
    pieces = 4
    piece = point_rows // pieces
    dual_rows = shard_rows // LANES
    block = shard_rows // SUM_BLOCKS
    group_rows = [shard_rows * part // sum(GROUP_PARTS) for part in GROUP_PARTS]
    starts = [sum(group_rows[:i]) for i in range(len(group_rows))]
    half_rows = shard_rows // 2
    target = point_rows * replicas / shard_rows
    inverse_soft = 1.0 / (features * softness_factor)
    routes = owners_ref.shape[0]

    me = lax.axis_index("cent")
    z = lax.axis_index("rep")
    core = me % 2
    xpos = (me // 2) % 2
    ypos = me // 4

    def rel(direction):
        dc, dx, dy = direction % 2, (direction // 2) % 2, direction // 4
        c = 1 - core if dc else core
        x = 1 - xpos if dx else xpos
        y = 1 - ypos if dy else ypos
        return (y * 2 + x) * 2 + c

    peer = [rel(d) for d in range(shards)]
    zpeer = [(z + k) % replicas for k in range(replicas)]

    at_end = jnp.logical_or(z == 0, z == replicas - 1)
    in_mid = jnp.logical_not(at_end)
    partner = z + 1 - 2 * (z % 2)
    middle = replicas - 1 - z

    barrier = pltpu.get_barrier_semaphore()
    for d in range(1, shards):
        pl.semaphore_signal(barrier, inc=1, device_id=(peer[d], z), device_id_type=MESH)
    for k in range(1, replicas):
        pl.semaphore_signal(barrier, inc=1, device_id=(me, zpeer[k]), device_id_type=MESH)

    def chunk_rows(slot, chunk, count=1):
        start = peer[slot] * point_rows + chunk * piece
        return pl.ds(pl.multiple_of(start, piece), piece * count)

    for step in (0, 2, 1, 3):
        units[chunk_rows(0, step), :] = normalize(points_ref[pl.ds(step * piece, piece), :])

    number = lax.broadcasted_iota(jnp.int32, (BLOCKS_DEV, point_rows), 0)
    named = []
    for r in range(routes):
        hit = blocks_ref[r, 0:1, :] == number
        for c in range(1, CAND):
            hit = jnp.logical_or(hit, blocks_ref[r, c : c + 1, :] == number)
        named.append(hit)
    for s in range(shards):
        marked = jnp.logical_and(owners_ref[0:1, :] == s, named[0])
        for r in range(1, routes):
            marked = jnp.logical_or(marked, jnp.logical_and(owners_ref[r : r + 1, :] == s, named[r]))
        marks_out[s] = jnp.where(marked, 1.0, 0.0)

    pl.semaphore_wait(barrier, shards - 1 + replicas - 1)

    unit_copies = {}

    def push(slot, chunk, direction):
        rows = chunk_rows(slot, chunk)
        copy = pltpu.make_async_remote_copy(
            src_ref=units.at[rows],
            dst_ref=units.at[rows],
            send_sem=unit_send.at[slot, chunk, direction // 2],
            recv_sem=unit_recv.at[slot ^ direction, chunk],
            device_id=(peer[direction], z),
            device_id_type=MESH,
        )
        copy.start()
        unit_copies[(slot, chunk, direction)] = copy

    def arrive(slot, chunk):
        rows = chunk_rows(slot, chunk)
        pltpu.make_async_copy(units.at[rows], units.at[rows], unit_recv.at[slot, chunk]).wait()

    order_x = (0, 1, 2, 3)
    order_y = (2, 3, 0, 1)
    push(0, 0, 2)
    push(0, 2, 4)
    mask_copies = []
    for d in range(1, shards):
        copy = pltpu.make_async_remote_copy(
            src_ref=marks_out.at[peer[d]],
            dst_ref=masks.at[me],
            send_sem=mask_send.at[d],
            recv_sem=mask_recv.at[d],
            device_id=(peer[d], z),
            device_id_type=MESH,
        )
        copy.start()
        mask_copies.append(copy)
    push(0, 1, 2)
    push(0, 3, 4)
    push(0, 2, 2)
    push(0, 0, 4)
    push(0, 3, 2)
    push(0, 1, 4)
    for step in range(pieces):
        push(0, step, 1)
    masks[me] = marks_out[me]

    cunit[...] = normalize(centroids_ref[...])

    def block_kernel(slot, chunk, count):
        held = chunk_rows(slot, chunk, count)
        scores = lax.dot_general(
            cunit[...],
            units[held, :],
            (((1,), (1,)), ((), ())),
            preferred_element_type=jnp.float32,
        )
        marks = masks[peer[slot], :, pl.ds(chunk * piece, count * piece)]
        for b in range(BLOCKS_DEV):
            kern[pl.ds(b * span, span), held] = (
                jnp.exp(scores[b * span : (b + 1) * span] * inverse_soft) * marks[b : b + 1, :]
            )

    def half_kernels(halves):
        for slot, chunks in halves:
            block_kernel(slot, min(chunks), 2)

    half_kernels(((0, (0, 1)), (0, (2, 3))))
    for step in range(pieces):
        tx, ty = order_x[step], order_y[step]
        arrive(2, tx)
        if step < 2:
            push(2, tx, 4)
        push(2, tx, 1)
        arrive(4, ty)
        if step < 2:
            push(4, ty, 2)
        push(4, ty, 1)
        if step == 1:
            for d in range(1, shards):
                pltpu.make_async_copy(
                    masks.at[peer[d]], masks.at[peer[d]], mask_recv.at[d]
                ).wait()
            for chunk in range(pieces):
                arrive(1, chunk)
            half_kernels(((1, (0, 1)), (1, (2, 3))))
        if step >= 2:
            arrive(6, order_x[step - 2])
            push(6, order_x[step - 2], 1)
            arrive(6, order_y[step - 2])
            push(6, order_y[step - 2], 1)
        if step == 2:
            for slot, chunks in ((3, order_x[:2]), (5, order_y[:2])):
                for chunk in chunks:
                    arrive(slot, chunk)
            half_kernels(((2, order_x[:2]), (4, order_y[:2]), (3, order_x[:2]), (5, order_y[:2])))
    half_kernels(((2, order_x[2:]), (4, order_y[2:])))
    for slot, chunks in ((3, order_x[2:]), (5, order_y[2:])):
        for chunk in chunks:
            arrive(slot, chunk)
        half_kernels(((slot, chunks),))
    half_kernels(((6, order_x[:2]), (6, order_y[:2])))
    for chunk in range(pieces):
        arrive(7, chunk)
    half_kernels(((7, order_x[:2]), (7, order_y[:2])))
    for copy in unit_copies.values():
        copy.wait_send()
    for copy in mask_copies:
        copy.wait_send()

    duals_now = jnp.concatenate([duals_ref[...]] * (SUBLANES // dual_rows), axis=0)
    groups = shard_rows // SUBLANES
    tiles = point_rows // LANES

    def slot_columns(p):
        return slice(p * point_rows, (p + 1) * point_rows)

    def spread_scale(scaling):
        for t in range(dual_rows):
            row = jnp.broadcast_to(scaling[t : t + 1, :], (LANES, LANES))
            scale_cols[pl.ds(t * LANES, LANES), :] = row.T

    def row_pass():
        def step(g, acc):
            rows = pl.ds(pl.multiple_of(g * SUBLANES, SUBLANES), SUBLANES)
            wide = jnp.concatenate([scale_cols[rows, :]] * tiles, axis=1)
            return tuple(acc[p] + kern[rows, slot_columns(p)] * wide for p in range(shards))

        zero = jnp.zeros((SUBLANES, point_rows), jnp.float32)
        acc = lax.fori_loop(0, groups, step, (zero,) * shards, unroll=2)
        return jnp.concatenate([jnp.sum(a, axis=0, keepdims=True) for a in acc], axis=0)

    def col_pass(inverse):
        wide = [
            jnp.broadcast_to(inverse[p : p + 1, :], (SUBLANES, point_rows)) for p in range(shards)
        ]

        def step(g, carry):
            rows = pl.ds(pl.multiple_of(g * SUBLANES, SUBLANES), SUBLANES)
            total = kern[rows, slot_columns(0)] * wide[0]
            for p in range(1, shards):
                total = total + kern[rows, slot_columns(p)] * wide[p]
            narrow = total[:, :LANES]
            for t in range(1, tiles):
                narrow = narrow + total[:, t * LANES : (t + 1) * LANES]
            mass_cols[rows, :] = narrow
            return carry

        lax.fori_loop(0, groups, step, 0, unroll=2)
        parts = [
            jnp.sum(mass_cols[pl.ds(t * LANES, LANES), :].T, axis=0, keepdims=True)
            for t in range(dual_rows)
        ]
        return jnp.concatenate(parts * (SUBLANES // dual_rows), axis=0)

    def row_exchange(turn, part):
        row_parts[turn, 0] = part.astype(row_parts.dtype)
        copies = []
        for d in (6, 7, 2, 4, 3, 5, 1):
            copy = pltpu.make_async_remote_copy(
                src_ref=row_parts.at[turn, 0],
                dst_ref=row_parts.at[turn, d],
                send_sem=row_send.at[turn, d],
                recv_sem=row_recv.at[turn, d],
                device_id=(peer[d], z),
                device_id_type=MESH,
            )
            copy.start()
            copies.append(copy)
        for copy in copies:
            copy.wait()
        total = part
        for d in range(1, shards):
            total = total + row_parts[turn, d].astype(jnp.float32)
        return total

    def col_exchange(turn, part):
        col_parts[turn, z] = part
        copies = []
        for k in range(1, replicas):
            copy = pltpu.make_async_remote_copy(
                src_ref=col_parts.at[turn, z],
                dst_ref=col_parts.at[turn, z],
                send_sem=col_send.at[turn, k],
                recv_sem=col_recv.at[turn, k],
                device_id=(me, zpeer[k]),
                device_id_type=MESH,
            )
            copy.start()
            copies.append(copy)
        for copy in copies:
            copy.wait()
        total = col_parts[turn, 0]
        for k in range(1, replicas):
            total = total + col_parts[turn, k]
        return total

    row_turn = 0
    col_turn = 0
    for loop_counter in range(ITERS):
        last = loop_counter == ITERS - 1
        for turn_index in range(SINK + 1):
            scaling = jnp.exp(duals_now)
            spread_scale(scaling)
            inverse = 1.0 / row_exchange(row_turn, row_pass())
            row_turn += 1
            if turn_index < SINK:
                mass = col_exchange(col_turn, col_pass(inverse) * scaling)
                col_turn += 1
                duals_now = duals_now + jnp.log(2.0 * target) - jnp.log(mass + target)

        dest = out_ref if last else cunit

        def raw_copy(i):
            rows = pl.ds(starts[i], group_rows[i])
            return pltpu.make_async_remote_copy(
                src_ref=raw_out.at[loop_counter, rows],
                dst_ref=raw_in.at[loop_counter, rows],
                send_sem=raw_send.at[loop_counter, i],
                recv_sem=raw_recv.at[loop_counter, i],
                device_id=(me, partner),
                device_id_type=MESH,
            )

        def pair_rows(i):
            return pl.ds(starts[i] // 2, group_rows[i] // 2)

        def pair_copy(i):
            return pltpu.make_async_remote_copy(
                src_ref=pair_out.at[loop_counter, pair_rows(i)],
                dst_ref=pair_in.at[loop_counter, pair_rows(i)],
                send_sem=pair_send.at[loop_counter, i],
                recv_sem=pair_recv.at[loop_counter, i],
                device_id=(me, middle),
                device_id_type=MESH,
            )

        def half_of(i, which):
            count = group_rows[i] // 2
            start = starts[i] + which * count
            if not isinstance(which, int):
                start = pl.multiple_of(start, 16)
            return pl.ds(start, count)

        def new_copy(i, which, to, number):
            return pltpu.make_async_remote_copy(
                src_ref=dest.at[half_of(i, which)],
                dst_ref=dest.at[half_of(i, which)],
                send_sem=new_send.at[loop_counter, i, number],
                recv_sem=new_recv.at[loop_counter, i, which],
                device_id=(me, to),
                device_id_type=MESH,
            )

        def new_arrive(i, which):
            ref = dest.at[half_of(i, which)]
            pltpu.make_async_copy(ref, ref, new_recv.at[loop_counter, i, which]).wait()

        own, other = z - 1, 2 - z

        def accumulate(j):
            rows = pl.ds(j * block, block)
            wide = jnp.concatenate([scale_cols[rows, :]] * tiles, axis=1)
            for p in range(shards):
                weights[:, slot_columns(p)] = (
                    inverse[p : p + 1, :] * kern[rows, slot_columns(p)] * wide
                ).astype(jnp.bfloat16)
            sums[rows, :] = jnp.dot(
                weights[...], units[...], preferred_element_type=jnp.float32
            )

            @pl.when(at_end)
            def _():
                raw_out[loop_counter, rows] = sums[rows, :].astype(jnp.bfloat16)
                for i in range(len(GROUP_PARTS)):
                    if j * block <= starts[i] < (j + 1) * block:
                        raw_copy(i).start()

        def pair_sums(i):
            @pl.when(in_mid)
            def _():
                raw_copy(i).wait_recv()
                rows = half_of(i, other)
                total = sums[rows, :] + raw_in[loop_counter, rows].astype(jnp.float32)
                pair_out[loop_counter, pair_rows(i)] = total.astype(jnp.bfloat16)
                pair_copy(i).start()

        def finish_sums(i):
            @pl.when(in_mid)
            def _():
                pair_copy(i).wait_recv()
                rows = half_of(i, own)
                total = sums[rows, :] + raw_in[loop_counter, rows].astype(jnp.float32)
                total = total + pair_in[loop_counter, pair_rows(i)].astype(jnp.float32)
                fresh = normalize(total)
                dest[rows, :] = fresh if last else normalize(fresh)
                new_copy(i, own, middle, 0).start()
                new_copy(i, own, partner, 1).start()

        def forward_new(i):
            @pl.when(in_mid)
            def _():
                new_arrive(i, other)
                new_copy(i, other, partner, 2).start()

        def end_new(i):
            @pl.when(at_end)
            def _():
                new_arrive(i, 0)
                new_arrive(i, 1)

        def remake(start, first, width):
            held = slice(first * point_rows, (first + width) * point_rows)
            scores = lax.dot_general(
                cunit[pl.ds(start, half_rows), :],
                units[held, :],
                (((1,), (1,)), ((), ())),
                preferred_element_type=jnp.float32,
            )
            for b in range(half_rows // span):
                line = start // span + b
                for p in range(width):
                    kern[pl.ds(start + b * span, span), slot_columns(first + p)] = (
                        jnp.exp(
                            scores[b * span : (b + 1) * span, slot_columns(p)] * inverse_soft
                        )
                        * masks[first + p, line : line + 1, :]
                    )

        count = len(GROUP_PARTS)
        early = [i for i in range(count) if starts[i] < half_rows]
        accumulate(0)
        accumulate(1)
        done = 2
        quarter = 0
        for step in range(count + 2):
            if step < count:
                pair_sums(step)
            if 0 <= step - 1 < count:
                finish_sums(step - 1)
            if 0 <= step - 2 < count:
                forward_new(step - 2)
            if done < SUM_BLOCKS:
                accumulate(done)
                done += 1
            if step - 2 >= len(early) - 1 and not last and quarter < 4:
                if quarter == 0:
                    for i in early:
                        end_new(i)
                remake(0, quarter * 2, 2)
                quarter += 1
        for i in range(count):
            if last or i not in early:
                end_new(i)
        if not last:
            remake(half_rows, 0, shards)
        for i in range(count):

            @pl.when(at_end)
            def _():
                raw_copy(i).wait_send()

            @pl.when(in_mid)
            def _():
                pair_copy(i).wait_send()
                new_copy(i, own, middle, 0).wait_send()
                new_copy(i, own, partner, 1).wait_send()
                new_copy(i, other, partner, 2).wait_send()

    duals_out_ref[...] = duals_now[:dual_rows]


def fused_body(points, centroids, owners, blocks, duals):
    point_rows, features = points.shape
    shard_rows = centroids.shape[0]
    shards = lax.axis_size("cent")
    replicas = lax.axis_size("rep")
    dims = (shards, replicas, point_rows, shard_rows, features)
    dual_rows = shard_rows // LANES
    dual_tile = duals.reshape(dual_rows, LANES)
    vmem = pl.BlockSpec(memory_space=pltpu.VMEM)
    row_turns = ITERS * (SINK + 1)
    col_turns = ITERS * SINK
    dma = pltpu.SemaphoreType.DMA
    count = len(GROUP_PARTS)
    new_centroids, duals_out = pl.pallas_call(
        functools.partial(fused_kernel, dims),
        out_shape=(
            jax.ShapeDtypeStruct((shard_rows, features), jnp.bfloat16),
            jax.ShapeDtypeStruct((dual_rows, LANES), jnp.float32),
        ),
        in_specs=[vmem] * 5,
        out_specs=(vmem, vmem),
        scratch_shapes=[
            pltpu.VMEM((shards * point_rows, features), jnp.bfloat16),
            pltpu.VMEM((shards, BLOCKS_DEV, point_rows), jnp.float32),
            pltpu.VMEM((shards, BLOCKS_DEV, point_rows), jnp.float32),
            pltpu.VMEM((shard_rows, shards * point_rows), jnp.float32),
            pltpu.VMEM((shard_rows, features), jnp.bfloat16),
            pltpu.VMEM((shard_rows, LANES), jnp.float32),
            pltpu.VMEM((shard_rows, LANES), jnp.float32),
            pltpu.VMEM((shard_rows // SUM_BLOCKS, shards * point_rows), jnp.bfloat16),
            pltpu.VMEM((shard_rows, features), jnp.float32),
            pltpu.VMEM((row_turns, shards, shards, point_rows), jnp.bfloat16),
            pltpu.VMEM((col_turns, replicas, SUBLANES, LANES), jnp.float32),
            pltpu.VMEM((ITERS, shard_rows, features), jnp.bfloat16),
            pltpu.VMEM((ITERS, shard_rows, features), jnp.bfloat16),
            pltpu.VMEM((ITERS, shard_rows // 2, features), jnp.bfloat16),
            pltpu.VMEM((ITERS, shard_rows // 2, features), jnp.bfloat16),
            dma((shards, 4, 3)),
            dma((shards, 4)),
            dma((shards,)),
            dma((shards,)),
            dma((row_turns, shards)),
            dma((row_turns, shards)),
            dma((col_turns, replicas)),
            dma((col_turns, replicas)),
            dma((ITERS, count)),
            dma((ITERS, count)),
            dma((ITERS, count)),
            dma((ITERS, count)),
            dma((ITERS, count, 3)),
            dma((ITERS, count, 2)),
        ],
        compiler_params=pltpu.CompilerParams(
            collective_id=0, has_side_effects=True, vmem_limit_bytes=VMEM_LIMIT
        ),
        name="fused_kmeans",
    )(points, centroids, owners.T, jnp.transpose(blocks, (1, 2, 0)), dual_tile)
    return new_centroids, duals_out.reshape(shard_rows)


def solution(mesh):
    shards = mesh.shape["cent"]

    def body(points, centroids, owners, blocks, duals):
        point_rows, features = points.shape
        shard_rows = centroids.shape[0]
        plane_bytes = shards * point_rows * (2 * features + 4 * shard_rows)
        cube = shards == 2**3 and mesh.shape["rep"] == 2 * 2 and shard_rows % (2 * SUBLANES * 2 * sum(GROUP_PARTS)) == 0 and SUBLANES % (shard_rows // LANES) == 0
        if cube and plane_bytes <= VMEM_LIMIT // 3:
            return fused_body(points, centroids, owners, blocks, duals)
        return routed_body(points, centroids, owners, blocks, duals)

    return jax.shard_map(
        body,
        mesh=mesh,
        in_specs=(
            P(("cent", "rep"), None),
            P("cent", None),
            P(("cent", "rep"), None),
            P(("cent", "rep"), None, None),
            P("cent"),
        ),
        out_specs=(P("cent", None), P("cent")),
        check_vma=False,
    )
```

```python
import functools

import jax
import jax.numpy as jnp
from jax import lax
from jax.experimental import pallas as pl
from jax.experimental.pallas import tpu as pltpu
from jax.sharding import PartitionSpec as P

BLOCKS_DEV = 8
CAND = 4
SINK = 3
ITERS = 2
LANES = 128
SUBLANES = 8
SUM_BLOCKS = 4
GROUP_PARTS = (2,) * 8
DELIVER = 2
MESH = pl.DeviceIdType.MESH
VMEM_LIMIT = 64000000


softness_factor = 0.02
EPSILON = 1e-06


def normalize(values):
    widened = values.astype(jnp.float32)
    return (
        widened * lax.rsqrt(jnp.mean(widened * widened, axis=-1, keepdims=True) + EPSILON)
    ).astype(jnp.bfloat16)


def candidate_mask(labels_in, block_span):
    member = jnp.any(
        labels_in[:, :, None] == jnp.arange(BLOCKS_DEV, dtype=jnp.int32)[None, None, :], axis=1
    )
    return jnp.repeat(member.astype(jnp.float32), block_span, axis=1)


def kernel_of(slot_rows, slot_mask, centroid_unit, feature_dimension):
    affinity_scores = lax.dot_general(
        slot_rows, centroid_unit, (((1,), (1,)), ((), ())), preferred_element_type=jnp.float32
    ) / (feature_dimension * softness_factor)
    return jnp.exp(affinity_scores) * slot_mask


def routed_body(points, centroids, owners, blocks, duals):
    point_rows, feature_dimension = points.shape
    shard_rows = centroids.shape[0]
    shards = lax.axis_size("cent")
    replicas = lax.axis_size("rep")
    routes = owners.shape[1]
    capacity = 5 * point_rows // shards
    block_span = shard_rows // BLOCKS_DEV
    target = point_rows * replicas / shard_rows
    unit_rows = normalize(points)
    flat_owner = owners.reshape(-1)
    flat_point = jnp.arange(point_rows * routes, dtype=jnp.int32) // routes
    onehot = (flat_owner[:, None] == jnp.arange(shards, dtype=jnp.int32)[None, :]).astype(jnp.int32)
    position = jnp.sum((jnp.cumsum(onehot, axis=0) - onehot) * onehot, axis=1)
    outgoing = (
        jnp.zeros((shards, capacity, feature_dimension), jnp.bfloat16)
        .at[flat_owner, position]
        .set(unit_rows[flat_point])
    )
    labels = (
        jnp.full((shards, capacity, CAND), -1, jnp.int32)
        .at[flat_owner, position]
        .set(blocks.reshape(-1, CAND))
    )
    first_unit = normalize(centroids)
    received_rows = (
        lax.all_to_all(outgoing, "cent", split_axis=0, concat_axis=0, tiled=True),
        lax.all_to_all(labels, "cent", split_axis=0, concat_axis=0, tiled=True),
    )
    slot_rows = received_rows[0].reshape(-1, feature_dimension)
    slot_mask = candidate_mask(received_rows[1].reshape(-1, CAND), block_span)
    first_kernel = kernel_of(slot_rows, slot_mask, first_unit, feature_dimension)
    current = centroids
    duals_now = duals
    for loop_counter in range(ITERS):
        if loop_counter == 0:
            kernel = first_kernel
        else:
            kernel = kernel_of(slot_rows, slot_mask, normalize(current), feature_dimension)
        for turn_index in range(SINK + 1):
            scaling = jnp.exp(duals_now)
            partial_rows = jnp.dot(kernel, scaling, precision=lax.Precision.HIGHEST).reshape(
                shards, capacity
            )
            returned = lax.all_to_all(partial_rows, "cent", split_axis=0, concat_axis=0, tiled=True)
            totals = jnp.sum(returned[flat_owner, position].reshape(point_rows, routes), axis=1)
            inverse = 1.0 / totals
            spread = (
                jnp.zeros((shards, capacity), jnp.float32)
                .at[flat_owner, position]
                .set(inverse[flat_point])
            )
            row_scale = lax.all_to_all(
                spread, "cent", split_axis=0, concat_axis=0, tiled=True
            ).reshape(-1)
            if turn_index < SINK:
                local_mass = jnp.dot(row_scale, kernel, precision=lax.Precision.HIGHEST) * scaling
                column_mass = lax.psum(local_mass, "rep")
                duals_now = duals_now + jnp.log(2.0 * target) - jnp.log(column_mass + target)
        weights = (row_scale[:, None] * kernel * scaling[None, :]).astype(jnp.bfloat16)
        share_sums = lax.psum_scatter(
            lax.dot_general(
                weights, slot_rows, (((0,), (0,)), ((), ())), preferred_element_type=jnp.float32
            ),
            "rep",
            scatter_dimension=0,
            tiled=True,
        )
        current = lax.all_gather(normalize(share_sums), "rep", axis=0, tiled=True)
    return (current, duals_now)


def fused_kernel(
    dims,
    points_ref,
    centroids_ref,
    owners_ref,
    blocks_ref,
    duals_ref,
    out_ref,
    duals_out_ref,
    units,
    marks_out,
    masks,
    kern,
    cunit,
    scale_cols,
    mass_cols,
    first_parts,
    weights,
    sums,
    row_parts,
    col_parts,
    raw_out,
    raw_in,
    pair_out,
    pair_in,
    unit_send,
    unit_recv,
    mask_send,
    mask_recv,
    row_send,
    row_recv,
    col_send,
    col_recv,
    raw_send,
    raw_recv,
    pair_send,
    pair_recv,
    new_send,
    new_recv,
    fetch,
):
    shards, replicas, point_rows, shard_rows, features = dims
    span = shard_rows // BLOCKS_DEV
    pieces = 4
    piece = point_rows // pieces
    dual_rows = shard_rows // LANES
    block = shard_rows // SUM_BLOCKS
    group_rows = [shard_rows * part // sum(GROUP_PARTS) for part in GROUP_PARTS]
    starts = [sum(group_rows[:i]) for i in range(len(group_rows))]
    half_rows = shard_rows // 2
    target = point_rows * replicas / shard_rows
    inverse_soft = 1.0 / (features * softness_factor)
    routes = owners_ref.shape[0]

    me = lax.axis_index("cent")
    z = lax.axis_index("rep")
    core = me % 2
    xpos = (me // 2) % 2
    ypos = me // 4

    def rel(direction):
        dc, dx, dy = direction % 2, (direction // 2) % 2, direction // 4
        c = 1 - core if dc else core
        x = 1 - xpos if dx else xpos
        y = 1 - ypos if dy else ypos
        return (y * 2 + x) * 2 + c

    peer = [rel(d) for d in range(shards)]
    zpeer = [(z + k) % replicas for k in range(replicas)]

    at_end = jnp.logical_or(z == 0, z == replicas - 1)
    in_mid = jnp.logical_not(at_end)
    partner = z + 1 - 2 * (z % 2)
    middle = replicas - 1 - z

    barrier = pltpu.get_barrier_semaphore()
    for d in range(1, shards):
        pl.semaphore_signal(barrier, inc=1, device_id=(peer[d], z), device_id_type=MESH)
    for k in range(1, replicas):
        pl.semaphore_signal(barrier, inc=1, device_id=(me, zpeer[k]), device_id_type=MESH)

    def chunk_rows(slot, chunk, count=1):
        start = peer[slot] * point_rows + chunk * piece
        return pl.ds(pl.multiple_of(start, piece), piece * count)

    held_points = units.at[chunk_rows(0, 0, pieces)]
    point_copy = pltpu.make_async_copy(points_ref, held_points, fetch.at[0])
    point_copy.start()
    centroid_copy = pltpu.make_async_copy(centroids_ref, cunit, fetch.at[1])
    centroid_copy.start()

    number = lax.broadcasted_iota(jnp.int32, (BLOCKS_DEV, point_rows), 0)
    named = []
    for r in range(routes):
        hit = blocks_ref[r, 0:1, :] == number
        for c in range(1, CAND):
            hit = jnp.logical_or(hit, blocks_ref[r, c : c + 1, :] == number)
        named.append(hit)
    for s in range(shards):
        marked = jnp.logical_and(owners_ref[0:1, :] == s, named[0])
        for r in range(1, routes):
            marked = jnp.logical_or(marked, jnp.logical_and(owners_ref[r : r + 1, :] == s, named[r]))
        marks_out[s] = jnp.where(marked, 1.0, 0.0)

    point_copy.wait()
    for step in (0, 2, 1, 3):
        units[chunk_rows(0, step), :] = normalize(units[chunk_rows(0, step), :])

    pl.semaphore_wait(barrier, shards - 1 + replicas - 1)

    unit_copies = {}

    def push(slot, chunk, direction):
        rows = chunk_rows(slot, chunk)
        copy = pltpu.make_async_remote_copy(
            src_ref=units.at[rows],
            dst_ref=units.at[rows],
            send_sem=unit_send.at[slot, chunk, direction // 2],
            recv_sem=unit_recv.at[slot ^ direction, chunk],
            device_id=(peer[direction], z),
            device_id_type=MESH,
        )
        copy.start()
        unit_copies[(slot, chunk, direction)] = copy

    def arrive(slot, chunk):
        rows = chunk_rows(slot, chunk)
        pltpu.make_async_copy(units.at[rows], units.at[rows], unit_recv.at[slot, chunk]).wait()

    order_x = (0, 1, 2, 3)
    order_y = (2, 3, 0, 1)
    push(0, 0, 2)
    push(0, 2, 4)
    mask_copies = []
    for d in range(1, shards):
        copy = pltpu.make_async_remote_copy(
            src_ref=marks_out.at[peer[d]],
            dst_ref=masks.at[me],
            send_sem=mask_send.at[d],
            recv_sem=mask_recv.at[d],
            device_id=(peer[d], z),
            device_id_type=MESH,
        )
        copy.start()
        mask_copies.append(copy)
    push(0, 1, 2)
    push(0, 3, 4)
    push(0, 2, 2)
    push(0, 0, 4)
    push(0, 3, 2)
    push(0, 1, 4)
    for step in range(pieces):
        push(0, step, 1)
    masks[me] = marks_out[me]

    centroid_copy.wait()
    cunit[...] = normalize(cunit[...])

    duals_now = jnp.concatenate([duals_ref[...]] * (SUBLANES // dual_rows), axis=0)

    def spread_scale(scaling):
        for t in range(dual_rows):
            row = jnp.broadcast_to(scaling[t : t + 1, :], (LANES, LANES))
            scale_cols[pl.ds(t * LANES, LANES), :] = row.T

    spread_scale(jnp.exp(duals_now))

    def fold(values, start):
        width = values.shape[1]
        wide = jnp.concatenate([scale_cols[pl.ds(start, span), :]] * (width // LANES), axis=1)
        scaled = (values * wide).reshape(span // SUBLANES, SUBLANES, width)
        return jnp.sum(scaled, axis=0)

    def block_kernel(slot, chunk, count):
        held = chunk_rows(slot, chunk, count)
        scores = lax.dot_general(
            cunit[...],
            units[held, :],
            (((1,), (1,)), ((), ())),
            preferred_element_type=jnp.float32,
        )
        marks = masks[peer[slot], :, pl.ds(chunk * piece, count * piece)]
        part = jnp.zeros((SUBLANES, count * piece), jnp.float32)
        for b in range(BLOCKS_DEV):
            values = jnp.exp(scores[b * span : (b + 1) * span] * inverse_soft) * marks[b : b + 1, :]
            kern[pl.ds(b * span, span), held] = values
            part = part + fold(values, b * span)
        first_parts[peer[slot], :, pl.ds(chunk * piece, count * piece)] = part

    def half_kernels(halves):
        for slot, chunks in halves:
            block_kernel(slot, min(chunks), 2)

    half_kernels(((0, (0, 1)), (0, (2, 3))))
    for step in range(pieces):
        tx, ty = order_x[step], order_y[step]
        arrive(2, tx)
        if step < 2:
            push(2, tx, 4)
        push(2, tx, 1)
        arrive(4, ty)
        if step < 2:
            push(4, ty, 2)
        push(4, ty, 1)
        if step == 1:
            for d in range(1, shards):
                pltpu.make_async_copy(
                    masks.at[peer[d]], masks.at[peer[d]], mask_recv.at[d]
                ).wait()
            for chunk in range(pieces):
                arrive(1, chunk)
            half_kernels(((1, (0, 1)), (1, (2, 3))))
        if step >= 2:
            arrive(6, order_x[step - 2])
            push(6, order_x[step - 2], 1)
            arrive(6, order_y[step - 2])
            push(6, order_y[step - 2], 1)
        if step == 2:
            for slot, chunks in ((3, order_x[:2]), (5, order_y[:2])):
                for chunk in chunks:
                    arrive(slot, chunk)
            half_kernels(((2, order_x[:2]), (4, order_y[:2]), (3, order_x[:2]), (5, order_y[:2])))
    half_kernels(((2, order_x[2:]), (4, order_y[2:])))
    for slot, chunks in ((3, order_x[2:]), (5, order_y[2:])):
        for chunk in chunks:
            arrive(slot, chunk)
        half_kernels(((slot, chunks),))
    half_kernels(((6, order_x[:2]), (6, order_y[:2])))
    for chunk in range(pieces):
        arrive(7, chunk)
    half_kernels(((7, order_x[:2]), (7, order_y[:2])))
    for copy in unit_copies.values():
        copy.wait_send()
    for copy in mask_copies:
        copy.wait_send()

    groups = shard_rows // SUBLANES
    tiles = point_rows // LANES

    def slot_columns(p):
        return slice(p * point_rows, (p + 1) * point_rows)

    def row_pass():
        def step(g, acc):
            rows = pl.ds(pl.multiple_of(g * SUBLANES, SUBLANES), SUBLANES)
            wide = jnp.concatenate([scale_cols[rows, :]] * tiles, axis=1)
            return tuple(acc[p] + kern[rows, slot_columns(p)] * wide for p in range(shards))

        zero = jnp.zeros((SUBLANES, point_rows), jnp.float32)
        acc = lax.fori_loop(0, groups, step, (zero,) * shards, unroll=2)
        return jnp.concatenate([jnp.sum(a, axis=0, keepdims=True) for a in acc], axis=0)

    def col_pass(inverse):
        wide = [
            jnp.broadcast_to(inverse[p : p + 1, :], (SUBLANES, point_rows)) for p in range(shards)
        ]

        def step(g, carry):
            rows = pl.ds(pl.multiple_of(g * SUBLANES, SUBLANES), SUBLANES)
            total = kern[rows, slot_columns(0)] * wide[0]
            for p in range(1, shards):
                total = total + kern[rows, slot_columns(p)] * wide[p]
            narrow = total[:, :LANES]
            for t in range(1, tiles):
                narrow = narrow + total[:, t * LANES : (t + 1) * LANES]
            mass_cols[rows, :] = narrow
            return carry

        lax.fori_loop(0, groups, step, 0, unroll=2)
        parts = [
            jnp.sum(mass_cols[pl.ds(t * LANES, LANES), :].T, axis=0, keepdims=True)
            for t in range(dual_rows)
        ]
        return jnp.concatenate(parts * (SUBLANES // dual_rows), axis=0)

    def row_exchange(turn, part):
        row_parts[turn, 0] = part.astype(row_parts.dtype)
        copies = []
        for d in (6, 7, 2, 4, 3, 5, 1):
            copy = pltpu.make_async_remote_copy(
                src_ref=row_parts.at[turn, 0],
                dst_ref=row_parts.at[turn, d],
                send_sem=row_send.at[turn, d],
                recv_sem=row_recv.at[turn, d],
                device_id=(peer[d], z),
                device_id_type=MESH,
            )
            copy.start()
            copies.append(copy)
        for copy in copies:
            copy.wait()
        total = part
        for d in range(1, shards):
            total = total + row_parts[turn, d].astype(jnp.float32)
        return total

    def col_exchange(turn, part):
        col_parts[turn, z] = part
        copies = []
        for k in range(1, replicas):
            copy = pltpu.make_async_remote_copy(
                src_ref=col_parts.at[turn, z],
                dst_ref=col_parts.at[turn, z],
                send_sem=col_send.at[turn, k],
                recv_sem=col_recv.at[turn, k],
                device_id=(me, zpeer[k]),
                device_id_type=MESH,
            )
            copy.start()
            copies.append(copy)
        for copy in copies:
            copy.wait()
        total = col_parts[turn, 0]
        for k in range(1, replicas):
            total = total + col_parts[turn, k]
        return total

    row_turn = 0
    col_turn = 0
    for loop_counter in range(ITERS):
        last = loop_counter == ITERS - 1
        for turn_index in range(SINK + 1):
            scaling = jnp.exp(duals_now)
            if turn_index == 0:
                part = jnp.concatenate(
                    [jnp.sum(first_parts[p], axis=0, keepdims=True) for p in range(shards)], axis=0
                )
            else:
                spread_scale(scaling)
                part = row_pass()
            inverse = 1.0 / row_exchange(row_turn, part)
            row_turn += 1
            if turn_index < SINK:
                mass = col_exchange(col_turn, col_pass(inverse) * scaling)
                col_turn += 1
                duals_now = duals_now + jnp.log(2.0 * target) - jnp.log(mass + target)

        dest = out_ref if last else cunit

        def raw_copy(i):
            rows = pl.ds(starts[i], group_rows[i])
            return pltpu.make_async_remote_copy(
                src_ref=raw_out.at[loop_counter, rows],
                dst_ref=raw_in.at[loop_counter, rows],
                send_sem=raw_send.at[loop_counter, i],
                recv_sem=raw_recv.at[loop_counter, i],
                device_id=(me, partner),
                device_id_type=MESH,
            )

        def pair_rows(i):
            return pl.ds(starts[i] // 2, group_rows[i] // 2)

        def pair_copy(i):
            return pltpu.make_async_remote_copy(
                src_ref=pair_out.at[loop_counter, pair_rows(i)],
                dst_ref=pair_in.at[loop_counter, pair_rows(i)],
                send_sem=pair_send.at[loop_counter, i],
                recv_sem=pair_recv.at[loop_counter, i],
                device_id=(me, middle),
                device_id_type=MESH,
            )

        def half_of(i, which):
            count = group_rows[i] // 2
            start = starts[i] + which * count
            if not isinstance(which, int):
                start = pl.multiple_of(start, 16)
            return pl.ds(start, count)

        def new_copy(i, which, to, number):
            return pltpu.make_async_remote_copy(
                src_ref=dest.at[half_of(i, which)],
                dst_ref=dest.at[half_of(i, which)],
                send_sem=new_send.at[loop_counter, i, number],
                recv_sem=new_recv.at[loop_counter, i, which],
                device_id=(me, to),
                device_id_type=MESH,
            )

        def new_arrive(i, which):
            ref = dest.at[half_of(i, which)]
            pltpu.make_async_copy(ref, ref, new_recv.at[loop_counter, i, which]).wait()

        own, other = z - 1, 2 - z

        def accumulate(j):
            rows = pl.ds(j * block, block)
            wide = jnp.concatenate([scale_cols[rows, :]] * tiles, axis=1)
            for p in range(shards):
                weights[:, slot_columns(p)] = (
                    inverse[p : p + 1, :] * kern[rows, slot_columns(p)] * wide
                ).astype(jnp.bfloat16)
            sums[rows, :] = jnp.dot(
                weights[...], units[...], preferred_element_type=jnp.float32
            )

            @pl.when(at_end)
            def _():
                raw_out[loop_counter, rows] = sums[rows, :].astype(jnp.bfloat16)
                for i in range(len(GROUP_PARTS)):
                    if j * block <= starts[i] < (j + 1) * block:
                        raw_copy(i).start()

        def pair_sums(i):
            @pl.when(in_mid)
            def _():
                raw_copy(i).wait_recv()
                rows = half_of(i, other)
                total = sums[rows, :] + raw_in[loop_counter, rows].astype(jnp.float32)
                pair_out[loop_counter, pair_rows(i)] = total.astype(jnp.bfloat16)
                pair_copy(i).start()

        def finish_sums(i):
            @pl.when(in_mid)
            def _():
                pair_copy(i).wait_recv()
                rows = half_of(i, own)
                total = sums[rows, :] + raw_in[loop_counter, rows].astype(jnp.float32)
                total = total + pair_in[loop_counter, pair_rows(i)].astype(jnp.float32)
                fresh = normalize(total)
                dest[rows, :] = fresh if last else normalize(fresh)
                new_copy(i, own, middle, 0).start()
                new_copy(i, own, partner, 1).start()

        def forward_new(i):
            @pl.when(in_mid)
            def _():
                new_arrive(i, other)
                new_copy(i, other, partner, 2).start()

        def end_new(i):
            @pl.when(at_end)
            def _():
                new_arrive(i, 0)
                new_arrive(i, 1)

        def remake(start, first, width):
            held = slice(first * point_rows, (first + width) * point_rows)
            scores = lax.dot_general(
                cunit[pl.ds(start, half_rows), :],
                units[held, :],
                (((1,), (1,)), ((), ())),
                preferred_element_type=jnp.float32,
            )
            for p in range(width):
                if start == 0:
                    part = jnp.zeros((SUBLANES, point_rows), jnp.float32)
                else:
                    part = first_parts[first + p]
                for b in range(half_rows // span):
                    line = start // span + b
                    values = (
                        jnp.exp(scores[b * span : (b + 1) * span, slot_columns(p)] * inverse_soft)
                        * masks[first + p, line : line + 1, :]
                    )
                    kern[pl.ds(start + b * span, span), slot_columns(first + p)] = values
                    part = part + fold(values, start + b * span)
                first_parts[first + p] = part

        count = len(GROUP_PARTS)
        early = [i for i in range(count) if starts[i] < half_rows]
        accumulate(0)
        accumulate(1)
        done = 2
        quarter = 0
        for step in range(count + 2):
            if step < count:
                pair_sums(step)
            if 0 <= step - 1 < count:
                finish_sums(step - 1)
            if 0 <= step - 2 < count:
                forward_new(step - 2)
            if done < SUM_BLOCKS:
                accumulate(done)
                done += 1
            if step - 2 >= len(early) - 1 and not last and quarter < 4:
                if quarter == 0:
                    for i in early:
                        end_new(i)
                remake(0, quarter * 2, 2)
                quarter += 1
        for i in range(count):
            if last or i not in early:
                end_new(i)
        if not last:
            remake(half_rows, 0, shards)
        for i in range(count):

            @pl.when(at_end)
            def _():
                raw_copy(i).wait_send()

            @pl.when(in_mid)
            def _():
                pair_copy(i).wait_send()
                new_copy(i, own, middle, 0).wait_send()
                new_copy(i, own, partner, 1).wait_send()
                new_copy(i, other, partner, 2).wait_send()

    duals_out_ref[...] = duals_now[:dual_rows]


def fused_body(points, centroids, owners, blocks, duals):
    point_rows, features = points.shape
    shard_rows = centroids.shape[0]
    shards = lax.axis_size("cent")
    replicas = lax.axis_size("rep")
    dims = (shards, replicas, point_rows, shard_rows, features)
    dual_rows = shard_rows // LANES
    dual_tile = duals.reshape(dual_rows, LANES)
    vmem = pl.BlockSpec(memory_space=pltpu.VMEM)
    hbm = pl.BlockSpec(memory_space=pltpu.HBM)
    row_turns = ITERS * (SINK + 1)
    col_turns = ITERS * SINK
    dma = pltpu.SemaphoreType.DMA
    count = len(GROUP_PARTS)
    new_centroids, duals_out = pl.pallas_call(
        functools.partial(fused_kernel, dims),
        out_shape=(
            jax.ShapeDtypeStruct((shard_rows, features), jnp.bfloat16),
            jax.ShapeDtypeStruct((dual_rows, LANES), jnp.float32),
        ),
        in_specs=[hbm, hbm, vmem, vmem, vmem],
        out_specs=(vmem, vmem),
        scratch_shapes=[
            pltpu.VMEM((shards * point_rows, features), jnp.bfloat16),
            pltpu.VMEM((shards, BLOCKS_DEV, point_rows), jnp.float32),
            pltpu.VMEM((shards, BLOCKS_DEV, point_rows), jnp.float32),
            pltpu.VMEM((shard_rows, shards * point_rows), jnp.float32),
            pltpu.VMEM((shard_rows, features), jnp.bfloat16),
            pltpu.VMEM((shard_rows, LANES), jnp.float32),
            pltpu.VMEM((shard_rows, LANES), jnp.float32),
            pltpu.VMEM((shards, SUBLANES, point_rows), jnp.float32),
            pltpu.VMEM((shard_rows // SUM_BLOCKS, shards * point_rows), jnp.bfloat16),
            pltpu.VMEM((shard_rows, features), jnp.float32),
            pltpu.VMEM((row_turns, shards, shards, point_rows), jnp.bfloat16),
            pltpu.VMEM((col_turns, replicas, SUBLANES, LANES), jnp.float32),
            pltpu.VMEM((ITERS, shard_rows, features), jnp.bfloat16),
            pltpu.VMEM((ITERS, shard_rows, features), jnp.bfloat16),
            pltpu.VMEM((ITERS, shard_rows // 2, features), jnp.bfloat16),
            pltpu.VMEM((ITERS, shard_rows // 2, features), jnp.bfloat16),
            dma((shards, 4, 3)),
            dma((shards, 4)),
            dma((shards,)),
            dma((shards,)),
            dma((row_turns, shards)),
            dma((row_turns, shards)),
            dma((col_turns, replicas)),
            dma((col_turns, replicas)),
            dma((ITERS, count)),
            dma((ITERS, count)),
            dma((ITERS, count)),
            dma((ITERS, count)),
            dma((ITERS, count, 3)),
            dma((ITERS, count, 2)),
            dma((2,)),
        ],
        compiler_params=pltpu.CompilerParams(
            collective_id=0, has_side_effects=True, vmem_limit_bytes=VMEM_LIMIT
        ),
        name="fused_kmeans",
    )(points, centroids, owners.T, jnp.transpose(blocks, (1, 2, 0)), dual_tile)
    new_centroids, duals_out = deliver(new_centroids, duals_out)
    return new_centroids, duals_out.reshape(shard_rows)


def deliver_kernel(rows_ref, line_ref, rows_out_ref, line_out_ref):
    rows_out_ref[...] = rows_ref[...]
    line_out_ref[...] = line_ref[...]


def deliver(rows, line):
    count, features = rows.shape
    tile = pl.BlockSpec((count // DELIVER, features), lambda i: (i, 0))
    whole = pl.BlockSpec(line.shape, lambda i: (0, 0))
    return pl.pallas_call(
        deliver_kernel,
        grid=(DELIVER,),
        out_shape=(
            jax.ShapeDtypeStruct(rows.shape, rows.dtype),
            jax.ShapeDtypeStruct(line.shape, line.dtype),
        ),
        in_specs=[tile, whole],
        out_specs=(tile, whole),
        name="deliver",
    )(rows, line)


def solution(mesh):
    shards = mesh.shape["cent"]

    def body(points, centroids, owners, blocks, duals):
        point_rows, features = points.shape
        shard_rows = centroids.shape[0]
        plane_bytes = shards * point_rows * (2 * features + 4 * shard_rows)
        cube = shards == 2**3 and mesh.shape["rep"] == 2 * 2 and shard_rows % (2 * SUBLANES * 2 * sum(GROUP_PARTS)) == 0 and SUBLANES % (shard_rows // LANES) == 0
        if cube and plane_bytes <= VMEM_LIMIT // 3:
            return fused_body(points, centroids, owners, blocks, duals)
        return routed_body(points, centroids, owners, blocks, duals)

    return jax.shard_map(
        body,
        mesh=mesh,
        in_specs=(
            P(("cent", "rep"), None),
            P("cent", None),
            P(("cent", "rep"), None),
            P(("cent", "rep"), None, None),
            P("cent"),
        ),
        out_specs=(P("cent", None), P("cent")),
        check_vma=False,
    )
```

```python
import functools

import jax
import jax.numpy as jnp
from jax import lax
from jax.experimental import pallas as pl
from jax.experimental.pallas import tpu as pltpu
from jax.sharding import PartitionSpec as P

BLOCKS_DEV = 8
CAND = 4
SINK = 3
ITERS = 2
LANES = 128
SUBLANES = 8
SUM_BLOCKS = 4
GROUP_PARTS = (2,) * 8
DELIVER = 2
MESH = pl.DeviceIdType.MESH
VMEM_LIMIT = 64000000


softness_factor = 0.02
EPSILON = 1e-06


def normalize(values):
    widened = values.astype(jnp.float32)
    return (
        widened * lax.rsqrt(jnp.mean(widened * widened, axis=-1, keepdims=True) + EPSILON)
    ).astype(jnp.bfloat16)


def candidate_mask(labels_in, block_span):
    member = jnp.any(
        labels_in[:, :, None] == jnp.arange(BLOCKS_DEV, dtype=jnp.int32)[None, None, :], axis=1
    )
    return jnp.repeat(member.astype(jnp.float32), block_span, axis=1)


def kernel_of(slot_rows, slot_mask, centroid_unit, feature_dimension):
    affinity_scores = lax.dot_general(
        slot_rows, centroid_unit, (((1,), (1,)), ((), ())), preferred_element_type=jnp.float32
    ) / (feature_dimension * softness_factor)
    return jnp.exp(affinity_scores) * slot_mask


def routed_body(points, centroids, owners, blocks, duals):
    point_rows, feature_dimension = points.shape
    shard_rows = centroids.shape[0]
    shards = lax.axis_size("cent")
    replicas = lax.axis_size("rep")
    routes = owners.shape[1]
    capacity = 5 * point_rows // shards
    block_span = shard_rows // BLOCKS_DEV
    target = point_rows * replicas / shard_rows
    unit_rows = normalize(points)
    flat_owner = owners.reshape(-1)
    flat_point = jnp.arange(point_rows * routes, dtype=jnp.int32) // routes
    onehot = (flat_owner[:, None] == jnp.arange(shards, dtype=jnp.int32)[None, :]).astype(jnp.int32)
    position = jnp.sum((jnp.cumsum(onehot, axis=0) - onehot) * onehot, axis=1)
    outgoing = (
        jnp.zeros((shards, capacity, feature_dimension), jnp.bfloat16)
        .at[flat_owner, position]
        .set(unit_rows[flat_point])
    )
    labels = (
        jnp.full((shards, capacity, CAND), -1, jnp.int32)
        .at[flat_owner, position]
        .set(blocks.reshape(-1, CAND))
    )
    first_unit = normalize(centroids)
    received_rows = (
        lax.all_to_all(outgoing, "cent", split_axis=0, concat_axis=0, tiled=True),
        lax.all_to_all(labels, "cent", split_axis=0, concat_axis=0, tiled=True),
    )
    slot_rows = received_rows[0].reshape(-1, feature_dimension)
    slot_mask = candidate_mask(received_rows[1].reshape(-1, CAND), block_span)
    first_kernel = kernel_of(slot_rows, slot_mask, first_unit, feature_dimension)
    current = centroids
    duals_now = duals
    for loop_counter in range(ITERS):
        if loop_counter == 0:
            kernel = first_kernel
        else:
            kernel = kernel_of(slot_rows, slot_mask, normalize(current), feature_dimension)
        for turn_index in range(SINK + 1):
            scaling = jnp.exp(duals_now)
            partial_rows = jnp.dot(kernel, scaling, precision=lax.Precision.HIGHEST).reshape(
                shards, capacity
            )
            returned = lax.all_to_all(partial_rows, "cent", split_axis=0, concat_axis=0, tiled=True)
            totals = jnp.sum(returned[flat_owner, position].reshape(point_rows, routes), axis=1)
            inverse = 1.0 / totals
            spread = (
                jnp.zeros((shards, capacity), jnp.float32)
                .at[flat_owner, position]
                .set(inverse[flat_point])
            )
            row_scale = lax.all_to_all(
                spread, "cent", split_axis=0, concat_axis=0, tiled=True
            ).reshape(-1)
            if turn_index < SINK:
                local_mass = jnp.dot(row_scale, kernel, precision=lax.Precision.HIGHEST) * scaling
                column_mass = lax.psum(local_mass, "rep")
                duals_now = duals_now + jnp.log(2.0 * target) - jnp.log(column_mass + target)
        weights = (row_scale[:, None] * kernel * scaling[None, :]).astype(jnp.bfloat16)
        share_sums = lax.psum_scatter(
            lax.dot_general(
                weights, slot_rows, (((0,), (0,)), ((), ())), preferred_element_type=jnp.float32
            ),
            "rep",
            scatter_dimension=0,
            tiled=True,
        )
        current = lax.all_gather(normalize(share_sums), "rep", axis=0, tiled=True)
    return (current, duals_now)


def fused_kernel(
    dims,
    points_ref,
    centroids_ref,
    owners_ref,
    blocks_ref,
    duals_ref,
    out_ref,
    duals_out_ref,
    units,
    marks_out,
    masks,
    kern,
    cunit,
    scale_cols,
    mass_cols,
    first_parts,
    weights,
    sums,
    row_parts,
    col_parts,
    raw_out,
    raw_in,
    pair_out,
    pair_in,
    unit_send,
    unit_recv,
    mask_send,
    mask_recv,
    row_send,
    row_recv,
    col_send,
    col_recv,
    raw_send,
    raw_recv,
    pair_send,
    pair_recv,
    new_send,
    new_recv,
    fetch,
):
    shards, replicas, point_rows, shard_rows, features = dims
    span = shard_rows // BLOCKS_DEV
    pieces = 4
    piece = point_rows // pieces
    dual_rows = shard_rows // LANES
    block = shard_rows // SUM_BLOCKS
    group_rows = [shard_rows * part // sum(GROUP_PARTS) for part in GROUP_PARTS]
    starts = [sum(group_rows[:i]) for i in range(len(group_rows))]
    half_rows = shard_rows // 2
    target = point_rows * replicas / shard_rows
    inverse_soft = 1.0 / (features * softness_factor)
    routes = owners_ref.shape[0]

    me = lax.axis_index("cent")
    z = lax.axis_index("rep")
    core = me % 2
    xpos = (me // 2) % 2
    ypos = me // 4

    def rel(direction):
        dc, dx, dy = direction % 2, (direction // 2) % 2, direction // 4
        c = 1 - core if dc else core
        x = 1 - xpos if dx else xpos
        y = 1 - ypos if dy else ypos
        return (y * 2 + x) * 2 + c

    peer = [rel(d) for d in range(shards)]
    zpeer = [(z + k) % replicas for k in range(replicas)]

    at_end = jnp.logical_or(z == 0, z == replicas - 1)
    in_mid = jnp.logical_not(at_end)
    partner = z + 1 - 2 * (z % 2)
    middle = replicas - 1 - z

    barrier = pltpu.get_barrier_semaphore()
    for d in range(1, shards):
        pl.semaphore_signal(barrier, inc=1, device_id=(peer[d], z), device_id_type=MESH)
    for k in range(1, replicas):
        pl.semaphore_signal(barrier, inc=1, device_id=(me, zpeer[k]), device_id_type=MESH)

    def chunk_rows(slot, chunk, count=1):
        start = peer[slot] * point_rows + chunk * piece
        return pl.ds(pl.multiple_of(start, piece), piece * count)

    held_points = units.at[chunk_rows(0, 0, pieces)]
    point_copy = pltpu.make_async_copy(points_ref, held_points, fetch.at[0])
    point_copy.start()
    centroid_copy = pltpu.make_async_copy(centroids_ref, cunit, fetch.at[1])
    centroid_copy.start()

    number = lax.broadcasted_iota(jnp.int32, (BLOCKS_DEV, point_rows), 0)
    named = []
    for r in range(routes):
        hit = blocks_ref[r, 0:1, :] == number
        for c in range(1, CAND):
            hit = jnp.logical_or(hit, blocks_ref[r, c : c + 1, :] == number)
        named.append(hit)
    for s in range(shards):
        marked = jnp.logical_and(owners_ref[0:1, :] == s, named[0])
        for r in range(1, routes):
            marked = jnp.logical_or(marked, jnp.logical_and(owners_ref[r : r + 1, :] == s, named[r]))
        marks_out[s] = jnp.where(marked, 1.0, 0.0)

    point_copy.wait()
    for step in (0, 2, 1, 3):
        units[chunk_rows(0, step), :] = normalize(units[chunk_rows(0, step), :])

    pl.semaphore_wait(barrier, shards - 1 + replicas - 1)

    unit_copies = {}

    def push(slot, chunk, direction):
        rows = chunk_rows(slot, chunk)
        copy = pltpu.make_async_remote_copy(
            src_ref=units.at[rows],
            dst_ref=units.at[rows],
            send_sem=unit_send.at[slot, chunk, direction // 2],
            recv_sem=unit_recv.at[slot ^ direction, chunk],
            device_id=(peer[direction], z),
            device_id_type=MESH,
        )
        copy.start()
        unit_copies[(slot, chunk, direction)] = copy

    def arrive(slot, chunk):
        rows = chunk_rows(slot, chunk)
        pltpu.make_async_copy(units.at[rows], units.at[rows], unit_recv.at[slot, chunk]).wait()

    order_x = (0, 1, 2, 3)
    order_y = (2, 3, 0, 1)
    push(0, 0, 2)
    push(0, 2, 4)
    mask_copies = []
    for d in range(1, shards):
        copy = pltpu.make_async_remote_copy(
            src_ref=marks_out.at[peer[d]],
            dst_ref=masks.at[me],
            send_sem=mask_send.at[d],
            recv_sem=mask_recv.at[d],
            device_id=(peer[d], z),
            device_id_type=MESH,
        )
        copy.start()
        mask_copies.append(copy)
    push(0, 1, 2)
    push(0, 3, 4)
    push(0, 2, 2)
    push(0, 0, 4)
    push(0, 3, 2)
    push(0, 1, 4)
    for step in range(pieces):
        push(0, step, 1)
    masks[me] = marks_out[me]

    centroid_copy.wait()
    cunit[...] = normalize(cunit[...])

    duals_now = jnp.concatenate([duals_ref[...]] * (SUBLANES // dual_rows), axis=0)

    def spread_scale(scaling):
        for t in range(dual_rows):
            row = jnp.broadcast_to(scaling[t : t + 1, :], (LANES, LANES))
            scale_cols[pl.ds(t * LANES, LANES), :] = row.T

    spread_scale(jnp.exp(duals_now))

    def fold(values, start):
        width = values.shape[1]
        wide = jnp.concatenate([scale_cols[pl.ds(start, span), :]] * (width // LANES), axis=1)
        scaled = (values * wide).reshape(span // SUBLANES, SUBLANES, width)
        return jnp.sum(scaled, axis=0)

    def block_kernel(slot, chunk, count):
        held = chunk_rows(slot, chunk, count)
        scores = lax.dot_general(
            cunit[...],
            units[held, :],
            (((1,), (1,)), ((), ())),
            preferred_element_type=jnp.float32,
        )
        marks = masks[peer[slot], :, pl.ds(chunk * piece, count * piece)]
        part = jnp.zeros((SUBLANES, count * piece), jnp.float32)
        for b in range(BLOCKS_DEV):
            values = jnp.exp(scores[b * span : (b + 1) * span] * inverse_soft) * marks[b : b + 1, :]
            kern[pl.ds(b * span, span), held] = values
            part = part + fold(values, b * span)
        first_parts[peer[slot], :, pl.ds(chunk * piece, count * piece)] = part

    def half_kernels(halves):
        for slot, chunks in halves:
            block_kernel(slot, min(chunks), 2)

    half_kernels(((0, (0, 1)), (0, (2, 3))))
    for step in range(pieces):
        tx, ty = order_x[step], order_y[step]
        arrive(2, tx)
        if step < 2:
            push(2, tx, 4)
        push(2, tx, 1)
        arrive(4, ty)
        if step < 2:
            push(4, ty, 2)
        push(4, ty, 1)
        if step == 1:
            for d in range(1, shards):
                pltpu.make_async_copy(
                    masks.at[peer[d]], masks.at[peer[d]], mask_recv.at[d]
                ).wait()
            for chunk in range(pieces):
                arrive(1, chunk)
            half_kernels(((1, (0, 1)), (1, (2, 3))))
        if step >= 2:
            arrive(6, order_x[step - 2])
            push(6, order_x[step - 2], 1)
            arrive(6, order_y[step - 2])
            push(6, order_y[step - 2], 1)
        if step == 2:
            for slot, chunks in ((3, order_x[:2]), (5, order_y[:2])):
                for chunk in chunks:
                    arrive(slot, chunk)
            half_kernels(((2, order_x[:2]), (4, order_y[:2]), (3, order_x[:2]), (5, order_y[:2])))
    half_kernels(((2, order_x[2:]), (4, order_y[2:])))
    for slot, chunks in ((3, order_x[2:]), (5, order_y[2:])):
        for chunk in chunks:
            arrive(slot, chunk)
        half_kernels(((slot, chunks),))
    half_kernels(((6, order_x[:2]), (6, order_y[:2])))
    for chunk in range(pieces):
        arrive(7, chunk)
    half_kernels(((7, order_x[:2]), (7, order_y[:2])))
    for copy in unit_copies.values():
        copy.wait_send()
    for copy in mask_copies:
        copy.wait_send()

    groups = shard_rows // SUBLANES
    tiles = point_rows // LANES

    def slot_columns(p):
        return slice(p * point_rows, (p + 1) * point_rows)

    def row_pass():
        def step(g, acc):
            rows = pl.ds(pl.multiple_of(g * SUBLANES, SUBLANES), SUBLANES)
            wide = jnp.concatenate([scale_cols[rows, :]] * tiles, axis=1)
            return tuple(acc[p] + kern[rows, slot_columns(p)] * wide for p in range(shards))

        zero = jnp.zeros((SUBLANES, point_rows), jnp.float32)
        acc = lax.fori_loop(0, groups, step, (zero,) * shards, unroll=2)
        return jnp.concatenate([jnp.sum(a, axis=0, keepdims=True) for a in acc], axis=0)

    def col_pass(inverse):
        wide = [
            jnp.broadcast_to(inverse[p : p + 1, :], (SUBLANES, point_rows)) for p in range(shards)
        ]

        def step(g, carry):
            rows = pl.ds(pl.multiple_of(g * SUBLANES, SUBLANES), SUBLANES)
            total = kern[rows, slot_columns(0)] * wide[0]
            for p in range(1, shards):
                total = total + kern[rows, slot_columns(p)] * wide[p]
            narrow = total[:, :LANES]
            for t in range(1, tiles):
                narrow = narrow + total[:, t * LANES : (t + 1) * LANES]
            mass_cols[rows, :] = narrow
            return carry

        lax.fori_loop(0, groups, step, 0, unroll=2)
        parts = [
            jnp.sum(mass_cols[pl.ds(t * LANES, LANES), :].T, axis=0, keepdims=True)
            for t in range(dual_rows)
        ]
        return jnp.concatenate(parts * (SUBLANES // dual_rows), axis=0)

    def row_exchange(turn, part):
        row_parts[turn, 0] = part.astype(row_parts.dtype)
        copies = []
        for d in (6, 7, 2, 4, 3, 5, 1):
            copy = pltpu.make_async_remote_copy(
                src_ref=row_parts.at[turn, 0],
                dst_ref=row_parts.at[turn, d],
                send_sem=row_send.at[turn, d],
                recv_sem=row_recv.at[turn, d],
                device_id=(peer[d], z),
                device_id_type=MESH,
            )
            copy.start()
            copies.append(copy)
        for copy in copies:
            copy.wait()
        total = part
        for d in range(1, shards):
            total = total + row_parts[turn, d].astype(jnp.float32)
        return total

    def col_exchange(turn, part):
        col_parts[turn, z] = part
        copies = []
        for k in range(1, replicas):
            copy = pltpu.make_async_remote_copy(
                src_ref=col_parts.at[turn, z],
                dst_ref=col_parts.at[turn, z],
                send_sem=col_send.at[turn, k],
                recv_sem=col_recv.at[turn, k],
                device_id=(me, zpeer[k]),
                device_id_type=MESH,
            )
            copy.start()
            copies.append(copy)
        for copy in copies:
            copy.wait()
        total = col_parts[turn, 0]
        for k in range(1, replicas):
            total = total + col_parts[turn, k]
        return total

    row_turn = 0
    col_turn = 0
    for loop_counter in range(ITERS):
        last = loop_counter == ITERS - 1
        for turn_index in range(SINK + 1):
            scaling = jnp.exp(duals_now)
            if turn_index == 0:
                part = jnp.concatenate(
                    [jnp.sum(first_parts[p], axis=0, keepdims=True) for p in range(shards)], axis=0
                )
            else:
                spread_scale(scaling)
                part = row_pass()
            inverse = 1.0 / row_exchange(row_turn, part)
            row_turn += 1
            if turn_index < SINK:
                mass = col_exchange(col_turn, col_pass(inverse) * scaling)
                col_turn += 1
                duals_now = duals_now + jnp.log(2.0 * target) - jnp.log(mass + target)

        dest = out_ref if last else cunit

        def raw_copy(i):
            rows = pl.ds(starts[i], group_rows[i])
            return pltpu.make_async_remote_copy(
                src_ref=raw_out.at[loop_counter, rows],
                dst_ref=raw_in.at[loop_counter, rows],
                send_sem=raw_send.at[loop_counter, i],
                recv_sem=raw_recv.at[loop_counter, i],
                device_id=(me, partner),
                device_id_type=MESH,
            )

        def pair_rows(i):
            return pl.ds(starts[i] // 2, group_rows[i] // 2)

        def pair_copy(i):
            return pltpu.make_async_remote_copy(
                src_ref=pair_out.at[loop_counter, pair_rows(i)],
                dst_ref=pair_in.at[loop_counter, pair_rows(i)],
                send_sem=pair_send.at[loop_counter, i],
                recv_sem=pair_recv.at[loop_counter, i],
                device_id=(me, middle),
                device_id_type=MESH,
            )

        def half_of(i, which):
            count = group_rows[i] // 2
            start = starts[i] + which * count
            if not isinstance(which, int):
                start = pl.multiple_of(start, 16)
            return pl.ds(start, count)

        def new_copy(i, which, to, number):
            return pltpu.make_async_remote_copy(
                src_ref=dest.at[half_of(i, which)],
                dst_ref=dest.at[half_of(i, which)],
                send_sem=new_send.at[loop_counter, i, number],
                recv_sem=new_recv.at[loop_counter, i, which],
                device_id=(me, to),
                device_id_type=MESH,
            )

        def new_arrive(i, which):
            ref = dest.at[half_of(i, which)]
            pltpu.make_async_copy(ref, ref, new_recv.at[loop_counter, i, which]).wait()

        own, other = z - 1, 2 - z

        def accumulate(j):
            rows = pl.ds(j * block, block)
            wide = jnp.concatenate([scale_cols[rows, :]] * tiles, axis=1)
            for p in range(shards):
                weights[:, slot_columns(p)] = (
                    inverse[p : p + 1, :] * kern[rows, slot_columns(p)] * wide
                ).astype(jnp.bfloat16)
            sums[rows, :] = jnp.dot(
                weights[...], units[...], preferred_element_type=jnp.float32
            )

            @pl.when(at_end)
            def _():
                raw_out[loop_counter, rows] = sums[rows, :].astype(jnp.bfloat16)
                for i in range(len(GROUP_PARTS)):
                    if j * block <= starts[i] < (j + 1) * block:
                        raw_copy(i).start()

        def pair_sums(i):
            @pl.when(in_mid)
            def _():
                raw_copy(i).wait_recv()
                rows = half_of(i, other)
                total = sums[rows, :] + raw_in[loop_counter, rows].astype(jnp.float32)
                pair_out[loop_counter, pair_rows(i)] = total.astype(jnp.bfloat16)
                pair_copy(i).start()

        def finish_sums(i):
            @pl.when(in_mid)
            def _():
                pair_copy(i).wait_recv()
                rows = half_of(i, own)
                total = sums[rows, :] + raw_in[loop_counter, rows].astype(jnp.float32)
                total = total + pair_in[loop_counter, pair_rows(i)].astype(jnp.float32)
                fresh = normalize(total)
                dest[rows, :] = fresh if last else normalize(fresh)
                new_copy(i, own, middle, 0).start()
                new_copy(i, own, partner, 1).start()

        def forward_new(i):
            @pl.when(in_mid)
            def _():
                new_arrive(i, other)
                new_copy(i, other, partner, 2).start()

        def end_new(i):
            @pl.when(at_end)
            def _():
                new_arrive(i, 0)
                new_arrive(i, 1)

        def remake(start, first, width):
            held = slice(first * point_rows, (first + width) * point_rows)
            scores = lax.dot_general(
                cunit[pl.ds(start, half_rows), :],
                units[held, :],
                (((1,), (1,)), ((), ())),
                preferred_element_type=jnp.float32,
            )
            for p in range(width):
                if start == 0:
                    part = jnp.zeros((SUBLANES, point_rows), jnp.float32)
                else:
                    part = first_parts[first + p]
                for b in range(half_rows // span):
                    line = start // span + b
                    values = (
                        jnp.exp(scores[b * span : (b + 1) * span, slot_columns(p)] * inverse_soft)
                        * masks[first + p, line : line + 1, :]
                    )
                    kern[pl.ds(start + b * span, span), slot_columns(first + p)] = values
                    part = part + fold(values, start + b * span)
                first_parts[first + p] = part

        count = len(GROUP_PARTS)
        early = [i for i in range(count) if starts[i] < half_rows]
        accumulate(0)
        accumulate(1)
        accumulate(2)
        done = 3
        quarter = 0
        for step in range(count + 2):
            if step < count:
                pair_sums(step)
            if 0 <= step - 1 < count:
                finish_sums(step - 1)
            if 0 <= step - 2 < count:
                forward_new(step - 2)
            if done < SUM_BLOCKS:
                accumulate(done)
                done += 1
            if step - 2 >= len(early) - 1 and not last and quarter < 4:
                if quarter == 0:
                    for i in early:
                        end_new(i)
                remake(0, quarter * 2, 2)
                quarter += 1
        for i in range(count):
            if last or i not in early:
                end_new(i)
        if not last:
            remake(half_rows, 0, shards)
        for i in range(count):

            @pl.when(at_end)
            def _():
                raw_copy(i).wait_send()

            @pl.when(in_mid)
            def _():
                pair_copy(i).wait_send()
                new_copy(i, own, middle, 0).wait_send()
                new_copy(i, own, partner, 1).wait_send()
                new_copy(i, other, partner, 2).wait_send()

    duals_out_ref[...] = duals_now[:dual_rows]


def fused_body(points, centroids, owners, blocks, duals):
    point_rows, features = points.shape
    shard_rows = centroids.shape[0]
    shards = lax.axis_size("cent")
    replicas = lax.axis_size("rep")
    dims = (shards, replicas, point_rows, shard_rows, features)
    dual_rows = shard_rows // LANES
    dual_tile = duals.reshape(dual_rows, LANES)
    vmem = pl.BlockSpec(memory_space=pltpu.VMEM)
    hbm = pl.BlockSpec(memory_space=pltpu.HBM)
    row_turns = ITERS * (SINK + 1)
    col_turns = ITERS * SINK
    dma = pltpu.SemaphoreType.DMA
    count = len(GROUP_PARTS)
    new_centroids, duals_out = pl.pallas_call(
        functools.partial(fused_kernel, dims),
        out_shape=(
            jax.ShapeDtypeStruct((shard_rows, features), jnp.bfloat16),
            jax.ShapeDtypeStruct((dual_rows, LANES), jnp.float32),
        ),
        in_specs=[hbm, hbm, vmem, vmem, vmem],
        out_specs=(vmem, vmem),
        scratch_shapes=[
            pltpu.VMEM((shards * point_rows, features), jnp.bfloat16),
            pltpu.VMEM((shards, BLOCKS_DEV, point_rows), jnp.float32),
            pltpu.VMEM((shards, BLOCKS_DEV, point_rows), jnp.float32),
            pltpu.VMEM((shard_rows, shards * point_rows), jnp.float32),
            pltpu.VMEM((shard_rows, features), jnp.bfloat16),
            pltpu.VMEM((shard_rows, LANES), jnp.float32),
            pltpu.VMEM((shard_rows, LANES), jnp.float32),
            pltpu.VMEM((shards, SUBLANES, point_rows), jnp.float32),
            pltpu.VMEM((shard_rows // SUM_BLOCKS, shards * point_rows), jnp.bfloat16),
            pltpu.VMEM((shard_rows, features), jnp.float32),
            pltpu.VMEM((row_turns, shards, shards, point_rows), jnp.bfloat16),
            pltpu.VMEM((col_turns, replicas, SUBLANES, LANES), jnp.float32),
            pltpu.VMEM((ITERS, shard_rows, features), jnp.bfloat16),
            pltpu.VMEM((ITERS, shard_rows, features), jnp.bfloat16),
            pltpu.VMEM((ITERS, shard_rows // 2, features), jnp.bfloat16),
            pltpu.VMEM((ITERS, shard_rows // 2, features), jnp.bfloat16),
            dma((shards, 4, 3)),
            dma((shards, 4)),
            dma((shards,)),
            dma((shards,)),
            dma((row_turns, shards)),
            dma((row_turns, shards)),
            dma((col_turns, replicas)),
            dma((col_turns, replicas)),
            dma((ITERS, count)),
            dma((ITERS, count)),
            dma((ITERS, count)),
            dma((ITERS, count)),
            dma((ITERS, count, 3)),
            dma((ITERS, count, 2)),
            dma((2,)),
        ],
        compiler_params=pltpu.CompilerParams(
            collective_id=0, has_side_effects=True, vmem_limit_bytes=VMEM_LIMIT
        ),
        name="fused_kmeans",
    )(points, centroids, owners.T, jnp.transpose(blocks, (1, 2, 0)), dual_tile)
    new_centroids, duals_out = deliver(new_centroids, duals_out)
    return new_centroids, duals_out.reshape(shard_rows)


def deliver_kernel(rows_ref, line_ref, rows_out_ref, line_out_ref):
    rows_out_ref[...] = rows_ref[...]
    line_out_ref[...] = line_ref[...]


def deliver(rows, line):
    count, features = rows.shape
    tile = pl.BlockSpec((count // DELIVER, features), lambda i: (i, 0))
    whole = pl.BlockSpec(line.shape, lambda i: (0, 0))
    return pl.pallas_call(
        deliver_kernel,
        grid=(DELIVER,),
        out_shape=(
            jax.ShapeDtypeStruct(rows.shape, rows.dtype),
            jax.ShapeDtypeStruct(line.shape, line.dtype),
        ),
        in_specs=[tile, whole],
        out_specs=(tile, whole),
        name="deliver",
    )(rows, line)


def solution(mesh):
    shards = mesh.shape["cent"]

    def body(points, centroids, owners, blocks, duals):
        point_rows, features = points.shape
        shard_rows = centroids.shape[0]
        plane_bytes = shards * point_rows * (2 * features + 4 * shard_rows)
        cube = shards == 2**3 and mesh.shape["rep"] == 2 * 2 and shard_rows % (2 * SUBLANES * 2 * sum(GROUP_PARTS)) == 0 and SUBLANES % (shard_rows // LANES) == 0
        if cube and plane_bytes <= VMEM_LIMIT // 3:
            return fused_body(points, centroids, owners, blocks, duals)
        return routed_body(points, centroids, owners, blocks, duals)

    return jax.shard_map(
        body,
        mesh=mesh,
        in_specs=(
            P(("cent", "rep"), None),
            P("cent", None),
            P(("cent", "rep"), None),
            P(("cent", "rep"), None, None),
            P("cent"),
        ),
        out_specs=(P("cent", None), P("cent")),
        check_vma=False,
    )
```
